32 devices in a mesh: dp: 16 (over z, y, core), expert: 2 (over x).
Axes of the slice: x: 2, y: 2, z: 4, core: 2. Of those that a mesh axis runs over, the one named last changes fastest.
Arguments:
- tokens: bfloat16 [4096, 2048], P(('dp', 'expert')), may hold values from -6 to 6
- cotangent: bfloat16 [4096, 2048], P(('dp', 'expert')), may hold values from -6 to 6
- expert_ids: int32 [4096, 8], P(('dp', 'expert')), may hold values from 0 to 127, as said below
- route_weights: float32 [4096, 8], P(('dp', 'expert')), may hold values from 0.1 to 1
- join_groups: int32 [16], replicated, may hold values from 0 to 1
- w_gate: bfloat16 [2048, 1024], P('dp', 'expert'), may hold values from -0.125 to 0.125
- w_up: bfloat16 [2048, 1024], P('dp', 'expert'), may hold values from -0.125 to 0.125
- w_down: bfloat16 [2048, 1024], P('dp', 'expert'), may hold values from -0.1875 to 0.1875
Outputs:
- mixed: bfloat16 [4096, 2048], P(('dp', 'expert'))
- grad_gate: bfloat16 [2048, 1024], P('dp', 'expert')
- grad_up: bfloat16 [2048, 1024], P('dp', 'expert')
- grad_down: bfloat16 [2048, 1024], P('dp', 'expert')
The draws below stay inside these ranges and needn't reach their ends.
Inputs may be any that keep to these rules, and one draw needn't show every extreme that they name: `expert_ids`: each row names 8 different experts; the rows of one device name expert 0 at most 16 times, and the rows of some device exactly 16 times.
All inputs are finite; a program needn't handle non-finite values.
Results may differ from the reference program's by a relative error of at most 0.014.
Values may be sent and summed in bfloat16 or wider, within the bound.
A program may use at most 64 MiB of HBM per device.

```python
import jax
import jax.numpy as jnp
from jax import lax

D = 2048
FF = 1024
NEXP_ALL = 128
TOP = 8
TOK_DEV = 128
CAP = 16
ROWS = 32
TOKENS = 4096
N_DP = 16
N_EXPERT = 2


def draw_expert_ids(key, part):
    key_count, key_pick, key_order, key_rest, key_turn = jax.random.split(key, 5)
    blocks = TOKENS // TOK_DEV
    counts = jax.random.randint(key_count, (blocks,), CAP // 4, CAP + 1)
    special = jax.random.randint(key_pick, (), 0, blocks)
    counts = jnp.where(jnp.arange(blocks) == special, CAP, counts)
    orders = jax.vmap(lambda sub_key: jax.random.permutation(sub_key, TOK_DEV))(jax.random.split(key_order, blocks))
    routed = (orders < counts[:, None]).reshape(TOKENS)
    scores = jax.random.randint(key_rest, (TOKENS, NEXP_ALL - 1), 0, 2 ** 30)
    others = 1 + jnp.argsort(scores, axis=-1)[:, :TOP]
    first = jnp.where(routed, 0, others[:, TOP - 1])
    chosen = jnp.concatenate([first[:, None], others[:, :TOP - 1]], axis=1)
    turns = jax.random.randint(key_turn, (TOKENS, 1), 0, TOP)
    index = (jnp.arange(TOP)[None, :] + turns) % TOP
    return jnp.take_along_axis(chosen, index, axis=1).astype(jnp.int32)


def set_ends(drawn, own_key, least, top_value):
    place = [jax.random.randint(jax.random.fold_in(own_key, axis), (), 0, length) for axis, length in enumerate(drawn.shape)]
    longest = drawn.shape.index(max(drawn.shape))
    next_to = place[:longest] + [(place[longest] + 1) % drawn.shape[longest]] + place[longest + 1:]
    return drawn.at[tuple(place)].set(least).at[tuple(next_to)].set(top_value)


def with_spikes(entries, rng, source, target, parts, factor):
    def block_of(dim):
        return (jnp.arange(entries.shape[dim]) // (entries.shape[dim] // parts)).reshape((-1,) + (1,) * (entries.ndim - 1 - dim))

    near = jax.random.permutation(rng, parts)[block_of(target)]
    second = (block_of(target) + parts // 2) % parts
    return jnp.where((block_of(source) == near) | (block_of(source) == second), factor * entries, entries)


def block_levels(own_key, shape, cuts, least, high):
    loudness, own = 1.0, jax.random.fold_in(own_key, 6)
    for dim, blocks in cuts:
        draws = jnp.exp(jax.random.uniform(jax.random.fold_in(own, dim), (blocks,), jnp.float32, least / len(cuts), high / len(cuts)))
        loudness = loudness * jnp.repeat(draws, shape[dim] // blocks).reshape([-1 if axis == dim else 1 for axis in range(len(shape))])
    return loudness


def scatter_about(key, extent, spread, bound, cuts=(), held_as=jnp.bfloat16):
    drawn = spread * jax.random.normal(key, extent, jnp.float32)
    if cuts:
        drawn = drawn * block_levels(key, extent, cuts, -0.22, 0.18)
    return jnp.clip(drawn, -bound, bound).astype(held_as)


def bell_draw_with(own_key, shape, spread, most, pieces, heavy, kind=jnp.bfloat16):
    values = spread * jax.random.normal(own_key, shape, jnp.float32)
    if pieces:
        values = values * block_levels(own_key, shape, pieces, -0.22, 0.18)
    return jnp.clip(with_spikes(values, jax.random.fold_in(own_key, 3), *heavy), -most, most).astype(kind)


def setup_inputs(seed: int = 0) -> dict:
    key_of = jax.random.split(jax.random.key(seed), 9)
    return {
        "tokens": bell_draw_with(key_of[0], (TOKENS, D), 1.0, 6.0, ((0, 32),), (0, 1, 32, 2.75)),
        "cotangent": bell_draw_with(key_of[1], (TOKENS, D), 1.0, 6.0, ((0, 32),), (0, 1, 32, 2.75)),
        "expert_ids": draw_expert_ids(jax.random.fold_in(key_of[8], 71), 0),
        "route_weights": jnp.clip(0.1 + 0.9 * jax.random.uniform(key_of[3], (TOKENS, TOP), jnp.float32) ** block_levels(key_of[3], (TOKENS, TOP), ((0, 32),), -0.2, 0.2), 0.1, 1.0),
        "join_groups": set_ends(jax.random.randint(key_of[4], (N_DP,), 0, 2), jax.random.fold_in(key_of[4], 1), 0, 1).astype(jnp.int32),
        "w_gate": scatter_about(key_of[5], (D, FF), D ** -0.5, 0.125, ((0, 16), (1, 2))),
        "w_up": scatter_about(key_of[6], (D, FF), D ** -0.5, 0.125, ((0, 16), (1, 2))),
        "w_down": scatter_about(key_of[7], (D, FF), FF ** -0.5, 0.1875, ((0, 16), (1, 2))),
    }


def reference(tokens, cotangent, expert_ids, route_weights, join_groups, w_gate, w_up, w_down):
    expert_count = N_EXPERT
    slice_width = FF // expert_count
    highest = lax.Precision.HIGHEST
    slot_ids = jnp.arange(CAP, dtype=jnp.int32)
    tok_groups = tokens.reshape(N_DP, expert_count, TOK_DEV, D)
    cot_groups = cotangent.reshape(N_DP, expert_count, TOK_DEV, D)
    id_groups = expert_ids.reshape(N_DP, expert_count, TOK_DEV, TOP)
    wt_groups = route_weights.reshape(N_DP, expert_count, TOK_DEV, TOP)

    def group_step(running, member):
        tok_block, cot_block, id_block, wt_block, joined = member
        chosen_mask = id_block == 0
        routed = jnp.any(chosen_mask, -1)
        weight = jnp.sum(jnp.where(chosen_mask, wt_block, 0.0), -1)
        places = jnp.cumsum(routed.astype(jnp.int32), -1) - 1
        chooser = ((places[:, None, :] == slot_ids[None, :, None]) & routed[:, None, :]).astype(jnp.float32)
        picked = jnp.einsum('ect,etd->ecd', chooser, tok_block.astype(jnp.float32), precision=highest)
        picked = picked.astype(jnp.bfloat16).reshape(ROWS, D)
        gate_acts = jnp.dot(picked, w_gate, preferred_element_type=jnp.float32)
        up_acts = jnp.dot(picked, w_up, preferred_element_type=jnp.float32)
        hidden = (jax.nn.silu(gate_acts) * up_acts).astype(jnp.bfloat16)
        partials = jnp.einsum('rjf,djf->jrd', hidden.reshape(ROWS, expert_count, slice_width).astype(jnp.float32),
                              w_down.reshape(D, expert_count, slice_width).astype(jnp.float32), precision=highest)
        out_rows = jnp.sum(partials.astype(jnp.bfloat16).astype(jnp.float32), 0).reshape(expert_count, CAP, D)
        mixed = jnp.einsum('ect,ecd->etd', chooser, out_rows, precision=highest) * weight[..., None]
        mixed = mixed.astype(jnp.bfloat16)
        scaled = cot_block.astype(jnp.float32) * weight[..., None]
        dpicked = jnp.einsum('ect,etd->ecd', chooser, scaled, precision=highest).astype(jnp.bfloat16).reshape(ROWS, D)
        hidden_grad = jnp.dot(dpicked, w_down, preferred_element_type=jnp.float32)
        sigma_gate = jax.nn.sigmoid(gate_acts)
        dgate = (hidden_grad * up_acts * sigma_gate * (1.0 + gate_acts * (1.0 - sigma_gate))).astype(jnp.bfloat16)
        dup = (hidden_grad * gate_acts * sigma_gate).astype(jnp.bfloat16)
        dims = (((0,), (0,)), ((), ()))
        term_gate = lax.dot_general(picked, dgate, dims, preferred_element_type=jnp.float32)
        term_up = lax.dot_general(picked, dup, dims, preferred_element_type=jnp.float32)
        term_down = lax.dot_general(dpicked, hidden, dims, preferred_element_type=jnp.float32)
        active = 1.0 - joined.astype(jnp.float32)
        running = running + active * jnp.stack([term_gate, term_up, term_down])
        return running, mixed

    start = jnp.zeros((3, D, FF), jnp.float32)
    sums, mixed_all = lax.scan(group_step, start, (tok_groups, cot_groups, id_groups, wt_groups, join_groups))
    return (mixed_all.reshape(TOKENS, D), sums[0].astype(jnp.bfloat16),
            sums[1].astype(jnp.bfloat16), sums[2].astype(jnp.bfloat16))
```

```python
import functools

import jax
import jax.numpy as jnp
from jax import lax
from jax.experimental import pallas as pl
from jax.experimental.pallas import tpu as pltpu
from jax.sharding import PartitionSpec as P

F32, BF16 = jnp.float32, jnp.bfloat16
MESH = pl.DeviceIdType.MESH


def dot(a, b, dims):
    return lax.dot_general(a, b, (dims, ((), ())), preferred_element_type=F32)


def kernel(
    pairs, members, cap,
    join, tok, cot, ids, wts, wg, wu, wd,
    mixed, grad_gate, grad_up, grad_down,
    wfull, blk, recv1, send2, recv2, acc, all3, send4, recv4, gacc, sendg, recvg,
    sw, rw, s1, r1, s2, r2, s3, r3, s4, r4, sg, rg,
):
    p, j = lax.axis_index("dp"), lax.axis_index("expert")
    pair, core = lax.div(p, 2), lax.rem(p, 2)
    total = pairs * members
    flat = pair * members + j
    partner = (2 * pair + 1 - core, j)
    tok_count = tok.shape[0]
    depth, width = wg.shape
    chip_depth = 2 * depth
    rows = members * cap

    def flat_peer(d):
        other = lax.rem(flat + d, total)
        return other, lax.div(other, members), lax.rem(other, members)

    def copy(src, dst, send, recv, device):
        return pltpu.make_async_remote_copy(
            src_ref=src, dst_ref=dst, send_sem=send, recv_sem=recv, device_id=device, device_id_type=MESH
        )

    barrier = pltpu.get_barrier_semaphore()

    def greet(d, carry):
        _, pair2, j2 = flat_peer(d)
        pl.semaphore_signal(barrier, inc=1, device_id=(2 * pair2 + core, j2), device_id_type=MESH)
        return carry

    lax.fori_loop(1, total, greet, 0)
    pl.semaphore_signal(barrier, inc=1, device_id=partner, device_id_type=MESH)

    chosen = ids[...] == 0
    routed = jnp.max(jnp.where(chosen, 1.0, 0.0), axis=1, keepdims=True)
    weight = jnp.sum(jnp.where(chosen, wts[...], 0.0), axis=1, keepdims=True)
    lower = lax.broadcasted_iota(jnp.int32, (tok_count, tok_count), 1) <= lax.broadcasted_iota(
        jnp.int32, (tok_count, tok_count), 0
    )
    wide = jnp.broadcast_to(routed, (tok_count, rows))
    places = dot(jnp.where(lower, 1.0, 0.0).astype(BF16), wide.astype(BF16), ((1,), (0,))) - 1.0
    slot = lax.rem(lax.broadcasted_iota(jnp.int32, (tok_count, rows), 1), cap).astype(F32)
    chooser = jnp.where((places == slot) & (wide > 0.5), 1.0, 0.0)
    chooser_half = chooser.astype(BF16)
    pick = chooser.T.astype(BF16)[:cap]
    active = 1.0 - join[p].astype(F32)
    scaled = (cot[...].astype(F32) * (weight * active)).astype(BF16)
    picked_rows = dot(pick, tok[...], ((1,), (0,))).astype(BF16)
    dpicked_rows = dot(pick, scaled, ((1,), (0,))).astype(BF16)
    for q in range(pairs):
        cols = slice(q * chip_depth, (q + 1) * chip_depth)
        blk[q, 0] = picked_rows[:, cols]
        blk[q, 1] = dpicked_rows[:, cols]

    pl.semaphore_wait(barrier, total)

    def start1(d, carry):
        _, pair2, j2 = flat_peer(d)
        copy(blk.at[pair2], recv1.at[flat], s1.at[d], r1.at[d], (2 * pair2 + core, j2)).start()
        return carry

    lax.fori_loop(1, total, start1, 0)
    weights = (wg, wu, wd)
    for n, w in enumerate(weights):
        copy(w, wfull.at[n, core], sw.at[n], rw.at[n], partner).start()
        wfull[n, core] = w[...]
    recv1[flat] = blk[pair]
    for n, w in enumerate(weights):
        copy(w, wfull.at[n, 1 - core], sw.at[n], rw.at[n], partner).wait_recv()

    def wait1(d, carry):
        copy(blk.at[0], recv1.at[lax.rem(flat - d + total, total)], s1.at[d], r1.at[d], partner).wait_recv()
        return carry

    lax.fori_loop(1, total, wait1, 0)

    picked = recv1[:, 0].reshape(total * cap, chip_depth)
    dpicked = recv1[:, 1].reshape(total * cap, chip_depth)
    full = [wfull[n].reshape(chip_depth, width) for n in range(3)]
    for n, left in enumerate((picked, picked, dpicked)):
        send2[:, n] = dot(left, full[n], ((1,), (0,))).astype(BF16).reshape(pairs, rows, width)

    def start2(d, carry):
        pair2 = lax.rem(pair + d, pairs)
        copy(send2.at[pair2], recv2.at[pair], s2.at[d], r2.at[d], (2 * pair2 + core, j)).start()
        return carry

    lax.fori_loop(1, pairs, start2, 0)
    acc[...] = send2[pair].astype(F32)

    def add2(d, carry):
        source = lax.rem(pair - d + pairs, pairs)
        copy(send2.at[0], recv2.at[source], s2.at[d], r2.at[d], partner).wait_recv()
        acc[...] += recv2[source].astype(F32)
        return carry

    lax.fori_loop(1, pairs, add2, 0)

    gate, up, dhidden = acc[0], acc[1], acc[2]
    sig = 1.0 / (1.0 + jnp.exp(-gate))
    all3[pair, 0] = (gate * sig * up).astype(BF16)
    all3[pair, 1] = (dhidden * up * sig * (1.0 + gate * (1.0 - sig))).astype(BF16)
    all3[pair, 2] = (dhidden * gate * sig).astype(BF16)

    def start3(d, carry):
        pair2 = lax.rem(pair + d, pairs)
        copy(all3.at[pair], all3.at[pair], s3.at[d], r3.at[d], (2 * pair2 + core, j)).start()
        return carry

    lax.fori_loop(1, pairs, start3, 0)

    def wait3(d, carry):
        source = lax.rem(pair - d + pairs, pairs)
        copy(all3.at[pair], all3.at[source], s3.at[d], r3.at[d], partner).wait_recv()
        return carry

    lax.fori_loop(1, pairs, wait3, 0)

    hidden, dgate, dup = (all3[:, n].reshape(pairs * rows, width) for n in range(3))
    send4[...] = dot(hidden, full[2], ((1,), (1,))).astype(BF16).reshape(total, cap, chip_depth)

    def start4(d, carry):
        other, pair2, j2 = flat_peer(d)
        copy(send4.at[other], recv4.at[j, pair], s4.at[d], r4.at[d], (2 * pair2 + core, j2)).start()
        return carry

    lax.fori_loop(1, total, start4, 0)
    recv4[j, pair] = send4[flat]

    for n, (left, right) in enumerate(((picked, dgate), (picked, dup), (dpicked, hidden))):
        term = dot(left, right, ((0,), (0,))).reshape(2, depth, width)
        gacc[n] = term
        sendg[n] = term.astype(BF16)
        copy(sendg.at[n, 1 - core], recvg.at[n], sg.at[n], rg.at[n], partner).start()

    def wait4(d, carry):
        source = lax.rem(flat - d + total, total)
        place = recv4.at[lax.rem(source, members), lax.div(source, members)]
        copy(send4.at[0], place, s4.at[d], r4.at[d], partner).wait_recv()
        return carry

    lax.fori_loop(1, total, wait4, 0)
    for q in range(pairs):
        part = recv4[:, q].reshape(rows, chip_depth)
        placed = dot(chooser_half, part, ((1,), (0,))) * weight
        mixed[:, q * chip_depth : (q + 1) * chip_depth] = placed.astype(BF16)

    for n, out in enumerate((grad_gate, grad_up, grad_down)):
        copy(sendg.at[n, 0], recvg.at[n], sg.at[n], rg.at[n], partner).wait_recv()
        out[...] = (gacc[n, core] + recvg[n].astype(F32)).astype(BF16)

    for n, w in enumerate(weights):
        copy(w, wfull.at[n, core], sw.at[n], rw.at[n], partner).wait_send()
        copy(sendg.at[n, 0], recvg.at[n], sg.at[n], rg.at[n], partner).wait_send()

    def drain_flat(d, carry):
        copy(blk.at[0], recv1.at[0], s1.at[d], r1.at[d], partner).wait_send()
        copy(send4.at[0], recv4.at[0, 0], s4.at[d], r4.at[d], partner).wait_send()
        return carry

    def drain_pair(d, carry):
        copy(send2.at[0], recv2.at[0], s2.at[d], r2.at[d], partner).wait_send()
        copy(all3.at[0], all3.at[0], s3.at[d], r3.at[d], partner).wait_send()
        return carry

    lax.fori_loop(1, total, drain_flat, 0)
    lax.fori_loop(1, pairs, drain_pair, 0)


def per_device(pairs, members, tokens, cotangent, expert_ids, route_weights, join_groups, w_gate, w_up, w_down):
    tok_count, model = tokens.shape
    depth, width = w_gate.shape
    cap = tok_count // 8
    total = pairs * members
    rows = members * cap
    vmem = pl.BlockSpec(memory_space=pltpu.VMEM)
    dma = pltpu.SemaphoreType.DMA
    grad = jax.ShapeDtypeStruct((depth, width), BF16)
    return pl.pallas_call(
        functools.partial(kernel, pairs, members, cap),
        out_shape=(jax.ShapeDtypeStruct((tok_count, model), BF16), grad, grad, grad),
        in_specs=[pl.BlockSpec(memory_space=pltpu.SMEM)] + [vmem] * 7,
        out_specs=(vmem,) * 4,
        scratch_shapes=[
            pltpu.VMEM((3, 2, depth, width), BF16),
            pltpu.VMEM((pairs, 2, cap, 2 * depth), BF16),
            pltpu.VMEM((total, 2, cap, 2 * depth), BF16),
            pltpu.VMEM((pairs, 3, rows, width), BF16),
            pltpu.VMEM((pairs, 3, rows, width), BF16),
            pltpu.VMEM((3, rows, width), F32),
            pltpu.VMEM((pairs, 3, rows, width), BF16),
            pltpu.VMEM((total, cap, 2 * depth), BF16),
            pltpu.VMEM((members, pairs, cap, 2 * depth), BF16),
            pltpu.VMEM((3, 2, depth, width), F32),
            pltpu.VMEM((3, 2, depth, width), BF16),
            pltpu.VMEM((3, depth, width), BF16),
            dma((3,)), dma((3,)),
            dma((total,)), dma((total,)),
            dma((pairs,)), dma((pairs,)),
            dma((pairs,)), dma((pairs,)),
            dma((total,)), dma((total,)),
            dma((3,)), dma((3,)),
        ],
        compiler_params=pltpu.CompilerParams(
            collective_id=0, has_side_effects=True, vmem_limit_bytes=48 * 1024 * 1024
        ),
        name="expert_step",
    )(join_groups, tokens, cotangent, expert_ids, route_weights, w_gate, w_up, w_down)


def solution(mesh):
    in_specs = (
        P(("dp", "expert"), None),
        P(("dp", "expert"), None),
        P(("dp", "expert"), None),
        P(("dp", "expert"), None),
        P(),
        P("dp", "expert"),
        P("dp", "expert"),
        P("dp", "expert"),
    )
    out_specs = (P(("dp", "expert"), None), P("dp", "expert"), P("dp", "expert"), P("dp", "expert"))
    body = functools.partial(per_device, mesh.shape["dp"] // 2, mesh.shape["expert"])
    return jax.shard_map(body, mesh=mesh, in_specs=in_specs, out_specs=out_specs, check_vma=False)
```

```python
import functools

import jax
import jax.numpy as jnp
from jax import lax
from jax.experimental import pallas as pl
from jax.experimental.pallas import tpu as pltpu
from jax.sharding import PartitionSpec as P

F32, BF16 = jnp.float32, jnp.bfloat16
MESH = pl.DeviceIdType.MESH


def dot(a, b, dims):
    return lax.dot_general(a, b, (dims, ((), ())), preferred_element_type=F32)


def kernel(
    pairs, members, cap,
    join, tok, cot, ids, wts, wg, wu, wd,
    mixed, grad_gate, grad_up, grad_down,
    tokv, cotv, wfull, blk, recv1, part, send2, recv_y, mid, recv_z, acc, all3, send4, recv4, gacc, sendg, recvg,
    local, sw, rw, s1, r1, s2y, r2y, s2z, r2z, s3y, r3y, s3z, r3z, s4, r4, sg, rg,
):
    p, j = lax.axis_index("dp"), lax.axis_index("expert")
    pair, core = lax.div(p, 2), lax.rem(p, 2)
    total = pairs * members
    flat = pair * members + j
    partner = (2 * pair + 1 - core, j)
    line, side = lax.div(pair, 2), lax.rem(pair, 2)
    lines = pairs // 2
    across = (2 * (2 * line + 1 - side) + core, j)
    last = lines - 1
    tok_count = tok.shape[0]
    depth, width = wg.shape
    chip_depth = 2 * depth
    rows = members * cap

    def flat_peer(d):
        other = lax.rem(flat + d, total)
        return other, lax.div(other, members), lax.rem(other, members)

    def copy(src, dst, send, recv, device):
        return pltpu.make_async_remote_copy(
            src_ref=src, dst_ref=dst, send_sem=send, recv_sem=recv, device_id=device, device_id_type=MESH
        )

    def on_line(other):
        return (2 * (2 * other + side) + core, j)

    weights = (wg, wu, wd)
    loads = [(cot, cotv), (tok, tokv)] + [(w, wfull.at[n, core]) for n, w in enumerate(weights)]
    loads = [pltpu.make_async_copy(src, dst, local.at[n]) for n, (src, dst) in enumerate(loads)]
    for load in loads:
        load.start()

    barrier = pltpu.get_barrier_semaphore()

    def greet(d, carry):
        _, pair2, j2 = flat_peer(d)
        pl.semaphore_signal(barrier, inc=1, device_id=(2 * pair2 + core, j2), device_id_type=MESH)
        return carry

    lax.fori_loop(1, total, greet, 0)
    pl.semaphore_signal(barrier, inc=1, device_id=partner, device_id_type=MESH)

    chosen = ids[...] == 0
    routed = jnp.max(jnp.where(chosen, 1.0, 0.0), axis=0, keepdims=True)
    weight = jnp.sum(jnp.where(chosen, wts[...], 0.0), axis=0, keepdims=True)
    upper = lax.broadcasted_iota(jnp.int32, (tok_count, tok_count), 0) <= lax.broadcasted_iota(
        jnp.int32, (tok_count, tok_count), 1
    )
    wide = jnp.broadcast_to(routed, (cap, tok_count))
    places = dot(wide.astype(BF16), jnp.where(upper, 1.0, 0.0).astype(BF16), ((1,), (0,))) - 1.0
    slot = lax.broadcasted_iota(jnp.int32, (cap, tok_count), 0).astype(F32)
    pick = jnp.where((places == slot) & (wide > 0.5), 1.0, 0.0)
    slot_weight = jnp.sum(pick * weight, axis=1, keepdims=True)
    spread = pick.T.astype(BF16)
    pick = pick.astype(BF16)
    active = 1.0 - join[p].astype(F32)
    loads[0].wait()
    dpicked_rows = (dot(pick, cotv[...], ((1,), (0,))) * (slot_weight * active)).astype(BF16)
    loads[1].wait()
    picked_rows = dot(pick, tokv[...], ((1,), (0,))).astype(BF16)
    for q in range(pairs):
        cols = slice(q * chip_depth, (q + 1) * chip_depth)
        blk[q, 0] = picked_rows[:, cols]
        blk[q, 1] = dpicked_rows[:, cols]

    pl.semaphore_wait(barrier, total)

    def start1(d, carry):
        _, pair2, j2 = flat_peer(d)
        copy(blk.at[pair2], recv1.at[flat], s1.at[d], r1.at[d], (2 * pair2 + core, j2)).start()
        return carry

    lax.fori_loop(1, total, start1, 0)
    for n, w in enumerate(weights):
        copy(w, wfull.at[n, core], sw.at[n], rw.at[n], partner).start()
    recv1[flat] = blk[pair]
    for n, w in enumerate(weights):
        loads[2 + n].wait()
        copy(w, wfull.at[n, 1 - core], sw.at[n], rw.at[n], partner).wait_recv()

    def wait1(d, carry):
        copy(blk.at[0], recv1.at[lax.rem(flat - d + total, total)], s1.at[d], r1.at[d], partner).wait_recv()
        return carry

    lax.fori_loop(1, total, wait1, 0)

    picked = recv1[:, 0].reshape(total * cap, chip_depth)
    dpicked = recv1[:, 1].reshape(total * cap, chip_depth)
    full = [wfull[n].reshape(chip_depth, width) for n in range(3)]
    for n, left in enumerate((picked, picked, dpicked)):
        term = dot(left, full[n], ((1,), (0,))).reshape(pairs, rows, width)
        part[:, n] = term
        send2[:, n] = term.astype(BF16)

    def start2(d, carry):
        other = lax.rem(line + 1 + d, lines)
        copy(send2.at[2 * other + 1 - side], recv_y.at[other], s2y.at[d], r2y.at[d], across).start()
        return carry

    lax.fori_loop(0, lines, start2, 0)

    def pass2(d, carry):
        other = lax.rem(line + 1 + d, lines)
        copy(send2.at[0], recv_y.at[other], s2y.at[d], r2y.at[d], across).wait_recv()
        mid[other] = (part[2 * other + side] + recv_y[other].astype(F32)).astype(BF16)
        copy(mid.at[other], recv_z.at[line], s2z.at[d], r2z.at[d], on_line(other)).start()
        return carry

    lax.fori_loop(0, last, pass2, 0)
    copy(send2.at[0], recv_y.at[line], s2y.at[last], r2y.at[last], across).wait_recv()
    acc[...] = part[pair] + recv_y[line].astype(F32)

    def add2(d, carry):
        source = lax.rem(line + last - d, lines)
        copy(mid.at[0], recv_z.at[source], s2z.at[d], r2z.at[d], across).wait_recv()
        acc[...] += recv_z[source].astype(F32)
        return carry

    lax.fori_loop(0, last, add2, 0)

    gate, up, dhidden = acc[0], acc[1], acc[2]
    sig = 1.0 / (1.0 + jnp.exp(-gate))
    all3[pair, 0] = (gate * sig * up).astype(BF16)
    all3[pair, 1] = (dhidden * up * sig * (1.0 + gate * (1.0 - sig))).astype(BF16)
    all3[pair, 2] = (dhidden * gate * sig).astype(BF16)

    copy(all3.at[pair], all3.at[pair], s3y.at[last], r3y.at[last], across).start()

    def start3(d, carry):
        other = lax.rem(line + 1 + d, lines)
        copy(all3.at[pair], all3.at[pair], s3z.at[d], r3z.at[d], on_line(other)).start()
        return carry

    lax.fori_loop(0, last, start3, 0)

    def pass3(d, carry):
        held = all3.at[2 * lax.rem(line + last - d, lines) + side]
        copy(all3.at[pair], held, s3z.at[d], r3z.at[d], across).wait_recv()
        copy(held, held, s3y.at[d], r3y.at[d], across).start()
        return carry

    lax.fori_loop(0, last, pass3, 0)

    def wait3(d, carry):
        source = lax.rem(line + last - d, lines)
        place = all3.at[2 * source + 1 - side]
        copy(all3.at[pair], place, s3y.at[d], r3y.at[d], across).wait_recv()
        return carry

    lax.fori_loop(0, last, wait3, 0)
    copy(all3.at[pair], all3.at[2 * line + 1 - side], s3y.at[last], r3y.at[last], across).wait_recv()

    hidden, dgate, dup = (all3[:, n].reshape(pairs * rows, width) for n in range(3))
    send4[...] = dot(hidden, full[2], ((1,), (1,))).astype(BF16).reshape(total, cap, chip_depth)

    def start4(d, carry):
        other, pair2, j2 = flat_peer(d)
        copy(send4.at[other], recv4.at[j, pair], s4.at[d], r4.at[d], (2 * pair2 + core, j2)).start()
        return carry

    lax.fori_loop(1, total, start4, 0)
    recv4[j, pair] = send4[flat]

    for n, (left, right) in enumerate(((picked, dgate), (picked, dup), (dpicked, hidden))):
        term = dot(left, right, ((0,), (0,))).reshape(2, depth, width)
        gacc[n] = term
        sendg[n] = term.astype(BF16)
        copy(sendg.at[n, 1 - core], recvg.at[n], sg.at[n], rg.at[n], partner).start()

    def wait4(d, carry):
        source = lax.rem(flat - d + total, total)
        place = recv4.at[lax.rem(source, members), lax.div(source, members)]
        copy(send4.at[0], place, s4.at[d], r4.at[d], partner).wait_recv()
        return carry

    lax.fori_loop(1, total, wait4, 0)
    for q in range(pairs):
        out_rows = recv4[0, q].astype(F32)
        for m in range(1, members):
            out_rows += recv4[m, q].astype(F32)
        placed = dot(spread, (out_rows * slot_weight).astype(BF16), ((1,), (0,)))
        mixed[:, q * chip_depth : (q + 1) * chip_depth] = placed.astype(BF16)

    for n, out in enumerate((grad_gate, grad_up, grad_down)):
        copy(sendg.at[n, 0], recvg.at[n], sg.at[n], rg.at[n], partner).wait_recv()
        out[...] = (gacc[n, core] + recvg[n].astype(F32)).astype(BF16)

    for n, w in enumerate(weights):
        copy(w, wfull.at[n, core], sw.at[n], rw.at[n], partner).wait_send()
        copy(sendg.at[n, 0], recvg.at[n], sg.at[n], rg.at[n], partner).wait_send()

    def drain_flat(d, carry):
        copy(blk.at[0], recv1.at[0], s1.at[d], r1.at[d], partner).wait_send()
        copy(send4.at[0], recv4.at[0, 0], s4.at[d], r4.at[d], partner).wait_send()
        return carry

    def drain_y(d, carry):
        copy(send2.at[0], recv_y.at[0], s2y.at[d], r2y.at[d], across).wait_send()
        copy(all3.at[0], all3.at[0], s3y.at[d], r3y.at[d], across).wait_send()
        return carry

    def drain_z(d, carry):
        copy(mid.at[0], recv_z.at[0], s2z.at[d], r2z.at[d], across).wait_send()
        copy(all3.at[0], all3.at[0], s3z.at[d], r3z.at[d], across).wait_send()
        return carry

    lax.fori_loop(1, total, drain_flat, 0)
    lax.fori_loop(0, lines, drain_y, 0)
    lax.fori_loop(0, last, drain_z, 0)


def per_device(pairs, members, tokens, cotangent, expert_ids, route_weights, join_groups, w_gate, w_up, w_down):
    tok_count, model = tokens.shape
    depth, width = w_gate.shape
    cap = tok_count // 8
    total = pairs * members
    rows = members * cap
    vmem = pl.BlockSpec(memory_space=pltpu.VMEM)
    hbm = pl.BlockSpec(memory_space=pl.ANY)
    lines = pairs // 2
    dma = pltpu.SemaphoreType.DMA
    grad = jax.ShapeDtypeStruct((depth, width), BF16)
    return pl.pallas_call(
        functools.partial(kernel, pairs, members, cap),
        out_shape=(jax.ShapeDtypeStruct((tok_count, model), BF16), grad, grad, grad),
        in_specs=[pl.BlockSpec(memory_space=pltpu.SMEM), hbm, hbm, vmem, vmem, hbm, hbm, hbm],
        out_specs=(vmem,) * 4,
        scratch_shapes=[
            pltpu.VMEM((tok_count, model), BF16),
            pltpu.VMEM((tok_count, model), BF16),
            pltpu.VMEM((3, 2, depth, width), BF16),
            pltpu.VMEM((pairs, 2, cap, 2 * depth), BF16),
            pltpu.VMEM((total, 2, cap, 2 * depth), BF16),
            pltpu.VMEM((pairs, 3, rows, width), F32),
            pltpu.VMEM((pairs, 3, rows, width), BF16),
            pltpu.VMEM((lines, 3, rows, width), BF16),
            pltpu.VMEM((lines, 3, rows, width), BF16),
            pltpu.VMEM((lines, 3, rows, width), BF16),
            pltpu.VMEM((3, rows, width), F32),
            pltpu.VMEM((pairs, 3, rows, width), BF16),
            pltpu.VMEM((total, cap, 2 * depth), BF16),
            pltpu.VMEM((members, pairs, cap, 2 * depth), BF16),
            pltpu.VMEM((3, 2, depth, width), F32),
            pltpu.VMEM((3, 2, depth, width), BF16),
            pltpu.VMEM((3, depth, width), BF16),
            dma((5,)),
            dma((3,)), dma((3,)),
            dma((total,)), dma((total,)),
            dma((lines,)), dma((lines,)),
            dma((lines,)), dma((lines,)),
            dma((lines,)), dma((lines,)),
            dma((lines,)), dma((lines,)),
            dma((total,)), dma((total,)),
            dma((3,)), dma((3,)),
        ],
        compiler_params=pltpu.CompilerParams(
            collective_id=0, has_side_effects=True, vmem_limit_bytes=60 * 1024 * 1024
        ),
        name="expert_step",
    )(join_groups, tokens, cotangent, expert_ids.T, route_weights.T, w_gate, w_up, w_down)


def solution(mesh):
    in_specs = (
        P(("dp", "expert"), None),
        P(("dp", "expert"), None),
        P(("dp", "expert"), None),
        P(("dp", "expert"), None),
        P(),
        P("dp", "expert"),
        P("dp", "expert"),
        P("dp", "expert"),
    )
    out_specs = (P(("dp", "expert"), None), P("dp", "expert"), P("dp", "expert"), P("dp", "expert"))
    body = functools.partial(per_device, mesh.shape["dp"] // 2, mesh.shape["expert"])
    return jax.shard_map(body, mesh=mesh, in_specs=in_specs, out_specs=out_specs, check_vma=False)
```

```python
import functools

import jax
import jax.numpy as jnp
from jax import lax
from jax.experimental import pallas as pl
from jax.experimental.pallas import tpu as pltpu
from jax.sharding import PartitionSpec as P

F32, BF16 = jnp.float32, jnp.bfloat16
MESH = pl.DeviceIdType.MESH
CHUNKS = 2


def dot(a, b, dims):
    return lax.dot_general(a, b, (dims, ((), ())), preferred_element_type=F32)


def kernel(
    pairs, members, cap,
    join, tok, cot, ids, wts, wg, wu, wd,
    mixed, grad_gate, grad_up, grad_down,
    tokv, cotv, wfull, blk, recv1, part, send2, recv_y, mid, recv_z, acc, all3, send4, recv4, gacc, sendg, recvg,
    local, sw, rw, s1, r1, s2y, r2y, s2z, r2z, s3y, r3y, s3z, r3z, s4, r4, sg, rg,
):
    p, j = lax.axis_index("dp"), lax.axis_index("expert")
    pair, core = lax.div(p, 2), lax.rem(p, 2)
    total = pairs * members
    flat = pair * members + j
    partner = (2 * pair + 1 - core, j)
    line, side = lax.div(pair, 2), lax.rem(pair, 2)
    lines = pairs // 2
    across = (2 * (2 * line + 1 - side) + core, j)
    last = lines - 1
    tok_count = tok.shape[0]
    depth, width = wg.shape
    chip_depth = 2 * depth
    rows = members * cap

    def flat_peer(d):
        other = lax.rem(flat + d, total)
        return other, lax.div(other, members), lax.rem(other, members)

    def copy(src, dst, send, recv, device):
        return pltpu.make_async_remote_copy(
            src_ref=src, dst_ref=dst, send_sem=send, recv_sem=recv, device_id=device, device_id_type=MESH
        )

    def on_line(other):
        return (2 * (2 * other + side) + core, j)

    weights = (wg, wu, wd)
    loads = [(cot, cotv), (tok, tokv)] + [(w, wfull.at[n, core]) for n, w in enumerate(weights)]
    loads = [pltpu.make_async_copy(src, dst, local.at[n]) for n, (src, dst) in enumerate(loads)]
    for load in loads:
        load.start()

    barrier = pltpu.get_barrier_semaphore()

    def greet(d, carry):
        _, pair2, j2 = flat_peer(d)
        pl.semaphore_signal(barrier, inc=1, device_id=(2 * pair2 + core, j2), device_id_type=MESH)
        return carry

    lax.fori_loop(1, total, greet, 0)
    pl.semaphore_signal(barrier, inc=1, device_id=partner, device_id_type=MESH)

    chosen = ids[...] == 0
    routed = jnp.max(jnp.where(chosen, 1.0, 0.0), axis=0, keepdims=True)
    weight = jnp.sum(jnp.where(chosen, wts[...], 0.0), axis=0, keepdims=True)
    upper = lax.broadcasted_iota(jnp.int32, (tok_count, tok_count), 0) <= lax.broadcasted_iota(
        jnp.int32, (tok_count, tok_count), 1
    )
    wide = jnp.broadcast_to(routed, (cap, tok_count))
    places = dot(wide.astype(BF16), jnp.where(upper, 1.0, 0.0).astype(BF16), ((1,), (0,))) - 1.0
    slot = lax.broadcasted_iota(jnp.int32, (cap, tok_count), 0).astype(F32)
    pick = jnp.where((places == slot) & (wide > 0.5), 1.0, 0.0)
    slot_weight = jnp.sum(pick * weight, axis=1, keepdims=True)
    spread = pick.T.astype(BF16)
    pick = pick.astype(BF16)
    active = 1.0 - join[p].astype(F32)
    loads[0].wait()
    dpicked_rows = (dot(pick, cotv[...], ((1,), (0,))) * (slot_weight * active)).astype(BF16)
    loads[1].wait()
    picked_rows = dot(pick, tokv[...], ((1,), (0,))).astype(BF16)
    for q in range(pairs):
        cols = slice(q * chip_depth, (q + 1) * chip_depth)
        blk[q, 0] = picked_rows[:, cols]
        blk[q, 1] = dpicked_rows[:, cols]

    pl.semaphore_wait(barrier, total)

    def start1(d, carry):
        _, pair2, j2 = flat_peer(d)
        copy(blk.at[pair2], recv1.at[flat], s1.at[d], r1.at[d], (2 * pair2 + core, j2)).start()
        return carry

    lax.fori_loop(1, total, start1, 0)
    for n, w in enumerate(weights):
        copy(w, wfull.at[n, core], sw.at[n], rw.at[n], partner).start()
    recv1[flat] = blk[pair]
    for n, w in enumerate(weights):
        loads[2 + n].wait()
        copy(w, wfull.at[n, 1 - core], sw.at[n], rw.at[n], partner).wait_recv()

    def wait1(d, carry):
        copy(blk.at[0], recv1.at[lax.rem(flat - d + total, total)], s1.at[d], r1.at[d], partner).wait_recv()
        return carry

    lax.fori_loop(1, total, wait1, 0)

    picked = recv1[:, 0].reshape(total * cap, chip_depth)
    dpicked = recv1[:, 1].reshape(total * cap, chip_depth)
    full = [wfull[n].reshape(chip_depth, width) for n in range(3)]
    for n, left in enumerate((picked, picked, dpicked)):
        term = dot(left, full[n], ((1,), (0,))).reshape(pairs, CHUNKS, rows // CHUNKS, width)
        for h in range(CHUNKS):
            part[h, :, n] = term[:, h]
            send2[h, :, n] = term[:, h].astype(BF16)

    def start2(h, d, carry):
        other, at = lax.rem(line + 1 + d, lines), h * lines + d
        copy(send2.at[h, 2 * other + 1 - side], recv_y.at[h, other], s2y.at[at], r2y.at[at], across).start()
        return carry

    def pass2(h, d, carry):
        other, at = lax.rem(line + 1 + d, lines), h * lines + d
        copy(send2.at[h, 0], recv_y.at[h, other], s2y.at[at], r2y.at[at], across).wait_recv()
        mid[h, other] = (part[h, 2 * other + side] + recv_y[h, other].astype(F32)).astype(BF16)
        copy(mid.at[h, other], recv_z.at[h, line], s2z.at[at], r2z.at[at], on_line(other)).start()
        return carry

    def add2(h, d, carry):
        source, at = lax.rem(line + last - d, lines), h * lines + d
        copy(mid.at[h, 0], recv_z.at[h, source], s2z.at[at], r2z.at[at], across).wait_recv()
        acc[h] += recv_z[h, source].astype(F32)
        return carry

    def start3(h, d, carry):
        other, at = lax.rem(line + 1 + d, lines), h * lines + d
        copy(all3.at[h, pair], all3.at[h, pair], s3z.at[at], r3z.at[at], on_line(other)).start()
        return carry

    def pass3(h, d, carry):
        at = h * lines + d
        held = all3.at[h, 2 * lax.rem(line + last - d, lines) + side]
        copy(all3.at[h, pair], held, s3z.at[at], r3z.at[at], across).wait_recv()
        copy(held, held, s3y.at[at], r3y.at[at], across).start()
        return carry

    def wait3(h, d, carry):
        at = h * lines + d
        place = all3.at[h, 2 * lax.rem(line + last - d, lines) + 1 - side]
        copy(all3.at[h, pair], place, s3y.at[at], r3y.at[at], across).wait_recv()
        return carry

    for h in range(CHUNKS):
        lax.fori_loop(0, lines, functools.partial(start2, h), 0)
    for h in range(CHUNKS):
        lax.fori_loop(0, last, functools.partial(pass2, h), 0)
        at = h * lines + last
        copy(send2.at[h, 0], recv_y.at[h, line], s2y.at[at], r2y.at[at], across).wait_recv()
        acc[h] = part[h, pair] + recv_y[h, line].astype(F32)
    for h in range(CHUNKS):
        lax.fori_loop(0, last, functools.partial(add2, h), 0)
        gate, up, dhidden = acc[h, 0], acc[h, 1], acc[h, 2]
        sig = 1.0 / (1.0 + jnp.exp(-gate))
        all3[h, pair, 0] = (gate * sig * up).astype(BF16)
        all3[h, pair, 1] = (dhidden * up * sig * (1.0 + gate * (1.0 - sig))).astype(BF16)
        all3[h, pair, 2] = (dhidden * gate * sig).astype(BF16)
        lax.fori_loop(0, last, functools.partial(start3, h), 0)
        at = h * lines + last
        copy(all3.at[h, pair], all3.at[h, pair], s3y.at[at], r3y.at[at], across).start()
    for h in range(CHUNKS):
        lax.fori_loop(0, last, functools.partial(pass3, h), 0)
    for h in range(CHUNKS):
        at = h * lines + last
        place = all3.at[h, 2 * line + 1 - side]
        copy(all3.at[h, pair], place, s3y.at[at], r3y.at[at], across).wait_recv()
        lax.fori_loop(0, last, functools.partial(wait3, h), 0)

    hidden, dgate, dup = (
        jnp.stack([all3[h, :, n] for h in range(CHUNKS)], axis=1).reshape(pairs * rows, width) for n in range(3)
    )
    send4[...] = dot(hidden, full[2], ((1,), (1,))).astype(BF16).reshape(total, cap, chip_depth)

    def start4(d, carry):
        other, pair2, j2 = flat_peer(d)
        copy(send4.at[other], recv4.at[j, pair], s4.at[d], r4.at[d], (2 * pair2 + core, j2)).start()
        return carry

    lax.fori_loop(1, total, start4, 0)
    recv4[j, pair] = send4[flat]

    for n, (left, right) in enumerate(((picked, dgate), (picked, dup), (dpicked, hidden))):
        term = dot(left, right, ((0,), (0,))).reshape(2, depth, width)
        gacc[n] = term
        sendg[n] = term.astype(BF16)
        copy(sendg.at[n, 1 - core], recvg.at[n], sg.at[n], rg.at[n], partner).start()

    def wait4(d, carry):
        source = lax.rem(flat - d + total, total)
        place = recv4.at[lax.rem(source, members), lax.div(source, members)]
        copy(send4.at[0], place, s4.at[d], r4.at[d], partner).wait_recv()
        return carry

    lax.fori_loop(1, total, wait4, 0)
    for q in range(pairs):
        out_rows = recv4[0, q].astype(F32)
        for m in range(1, members):
            out_rows += recv4[m, q].astype(F32)
        placed = dot(spread, (out_rows * slot_weight).astype(BF16), ((1,), (0,)))
        mixed[:, q * chip_depth : (q + 1) * chip_depth] = placed.astype(BF16)

    for n, out in enumerate((grad_gate, grad_up, grad_down)):
        copy(sendg.at[n, 0], recvg.at[n], sg.at[n], rg.at[n], partner).wait_recv()
        out[...] = (gacc[n, core] + recvg[n].astype(F32)).astype(BF16)

    for n, w in enumerate(weights):
        copy(w, wfull.at[n, core], sw.at[n], rw.at[n], partner).wait_send()
        copy(sendg.at[n, 0], recvg.at[n], sg.at[n], rg.at[n], partner).wait_send()

    def drain_flat(d, carry):
        copy(blk.at[0], recv1.at[0], s1.at[d], r1.at[d], partner).wait_send()
        copy(send4.at[0], recv4.at[0, 0], s4.at[d], r4.at[d], partner).wait_send()
        return carry

    def drain_y(d, carry):
        copy(send2.at[0, 0], recv_y.at[0, 0], s2y.at[d], r2y.at[d], across).wait_send()
        copy(all3.at[0, 0], all3.at[0, 0], s3y.at[d], r3y.at[d], across).wait_send()
        return carry

    def drain_z(h, d, carry):
        at = h * lines + d
        copy(mid.at[0, 0], recv_z.at[0, 0], s2z.at[at], r2z.at[at], across).wait_send()
        copy(all3.at[0, 0], all3.at[0, 0], s3z.at[at], r3z.at[at], across).wait_send()
        return carry

    lax.fori_loop(1, total, drain_flat, 0)
    lax.fori_loop(0, CHUNKS * lines, drain_y, 0)
    for h in range(CHUNKS):
        lax.fori_loop(0, last, functools.partial(drain_z, h), 0)


def per_device(pairs, members, tokens, cotangent, expert_ids, route_weights, join_groups, w_gate, w_up, w_down):
    tok_count, model = tokens.shape
    depth, width = w_gate.shape
    cap = tok_count // 8
    total = pairs * members
    rows = members * cap
    vmem = pl.BlockSpec(memory_space=pltpu.VMEM)
    hbm = pl.BlockSpec(memory_space=pl.ANY)
    lines = pairs // 2
    dma = pltpu.SemaphoreType.DMA
    grad = jax.ShapeDtypeStruct((depth, width), BF16)
    return pl.pallas_call(
        functools.partial(kernel, pairs, members, cap),
        out_shape=(jax.ShapeDtypeStruct((tok_count, model), BF16), grad, grad, grad),
        in_specs=[pl.BlockSpec(memory_space=pltpu.SMEM), hbm, hbm, vmem, vmem, hbm, hbm, hbm],
        out_specs=(vmem,) * 4,
        scratch_shapes=[
            pltpu.VMEM((tok_count, model), BF16),
            pltpu.VMEM((tok_count, model), BF16),
            pltpu.VMEM((3, 2, depth, width), BF16),
            pltpu.VMEM((pairs, 2, cap, 2 * depth), BF16),
            pltpu.VMEM((total, 2, cap, 2 * depth), BF16),
            pltpu.VMEM((CHUNKS, pairs, 3, rows // CHUNKS, width), F32),
            pltpu.VMEM((CHUNKS, pairs, 3, rows // CHUNKS, width), BF16),
            pltpu.VMEM((CHUNKS, lines, 3, rows // CHUNKS, width), BF16),
            pltpu.VMEM((CHUNKS, lines, 3, rows // CHUNKS, width), BF16),
            pltpu.VMEM((CHUNKS, lines, 3, rows // CHUNKS, width), BF16),
            pltpu.VMEM((CHUNKS, 3, rows // CHUNKS, width), F32),
            pltpu.VMEM((CHUNKS, pairs, 3, rows // CHUNKS, width), BF16),
            pltpu.VMEM((total, cap, 2 * depth), BF16),
            pltpu.VMEM((members, pairs, cap, 2 * depth), BF16),
            pltpu.VMEM((3, 2, depth, width), F32),
            pltpu.VMEM((3, 2, depth, width), BF16),
            pltpu.VMEM((3, depth, width), BF16),
            dma((5,)),
            dma((3,)), dma((3,)),
            dma((total,)), dma((total,)),
            dma((CHUNKS * lines,)), dma((CHUNKS * lines,)),
            dma((CHUNKS * lines,)), dma((CHUNKS * lines,)),
            dma((CHUNKS * lines,)), dma((CHUNKS * lines,)),
            dma((CHUNKS * lines,)), dma((CHUNKS * lines,)),
            dma((total,)), dma((total,)),
            dma((3,)), dma((3,)),
        ],
        compiler_params=pltpu.CompilerParams(
            collective_id=0, has_side_effects=True, vmem_limit_bytes=60 * 1024 * 1024
        ),
        name="expert_step",
    )(join_groups, tokens, cotangent, expert_ids.T, route_weights.T, w_gate, w_up, w_down)


def solution(mesh):
    in_specs = (
        P(("dp", "expert"), None),
        P(("dp", "expert"), None),
        P(("dp", "expert"), None),
        P(("dp", "expert"), None),
        P(),
        P("dp", "expert"),
        P("dp", "expert"),
        P("dp", "expert"),
    )
    out_specs = (P(("dp", "expert"), None), P("dp", "expert"), P("dp", "expert"), P("dp", "expert"))
    body = functools.partial(per_device, mesh.shape["dp"] // 2, mesh.shape["expert"])
    return jax.shard_map(body, mesh=mesh, in_specs=in_specs, out_specs=out_specs, check_vma=False)
```
